512 devices in a mesh: dp: 64 (over y, z), expert: 8 (over x, core).
Axes of the slice: x: 4, y: 4, z: 16, core: 2. Of those that a mesh axis runs over, the one named last changes fastest.
Arguments:
- tokens: bfloat16 [32768, 2048], P(('dp', 'expert')), may hold values from -16 to 16
- cotangent: bfloat16 [32768, 2048], P(('dp', 'expert')), may hold values from -8 to 8
- route: int32 [65536], P(('dp', 'expert')), may hold values from 0 to 63, as said below
- counts: int32 [512, 8], P(('dp', 'expert')), may hold values from 8 to 16, as said below
- gate_master: float32 [8, 2048, 768], P('expert', 'dp'), may hold values from -0.125 to 0.125
- up_master: float32 [8, 2048, 768], P('expert', 'dp'), may hold values from -0.125 to 0.125
- down_master: float32 [8, 2048, 768], P('expert', 'dp'), may hold values from -0.21875 to 0.21875
- first_moment: float32 [8, 3, 2048, 768], P('expert', None, 'dp'), may hold values from -2 to 2
- second_moment: float32 [8, 3, 2048, 768], P('expert', None, 'dp'), may hold values from 0.01 to 1
Outputs:
- combined: float32 [8, 3, 2048, 768], P('expert', None, 'dp')
- new_weights: float32 [8, 3, 2048, 768], P('expert', None, 'dp')
- new_first: float32 [8, 3, 2048, 768], P('expert', None, 'dp')
- new_second: float32 [8, 3, 2048, 768], P('expert', None, 'dp')
- forward: bfloat16 [32768, 2048], P(('dp', 'expert'))
The draws below stay inside these ranges and needn't reach their ends.
Inputs may be any that keep to these rules, and one draw needn't show every extreme that they name: `route`: for each device and each expert, the 16 slots name distinct local token rows. `counts`: in every draw, for some data index and some expert, every source device of that data index sends exactly 16 live slots.
All inputs are finite; a program needn't handle non-finite values.
Results may differ from the reference program's by a relative error of at most 0.011.
The reference program's roundings to bfloat16 on the way count: a program that leaves them out, or rounds other values in their place, can miss the bound.
Values may be sent and summed in bfloat16 or wider, within the bound.
A program may use at most 128 MiB of HBM per device.

```python
import math
import jax
import jax.numpy as jnp
from jax import lax

D = 2048
FF = 768
ROWS = 128
EXPERTS = 8
POOL = 64
CAP = 16
LEVELS = 6
ALL_TOKENS = 32768
N_DP = 64
N_EXPERT = 8


def feature_scales(key):
    values = jnp.exp(jax.random.uniform(key, (D,), jnp.float32, jnp.log(0.5), jnp.log(5.0)))
    return values / jnp.sqrt(jnp.mean(values * values))


def draw_tokens(key, part):
    total_rows = POOL * N_DP * N_EXPERT
    scales = feature_scales(jax.random.fold_in(key, 11))
    common = jax.random.normal(jax.random.fold_in(key, 12), (D,), jnp.float32)
    noise = jax.random.normal(jax.random.fold_in(key, 15), (total_rows, D), jnp.float32)
    values = (0.7 * common[None, :] + noise) * scales[None, :]
    return jnp.clip(values, -16.0, 16.0).astype(jnp.bfloat16)


def draw_cotangent(key, part):
    total_rows = POOL * N_DP * N_EXPERT
    scales = feature_scales(jax.random.fold_in(key, 31))
    common = jax.random.normal(jax.random.fold_in(key, 32), (D,), jnp.float32)
    data_pos = (jnp.arange(total_rows, dtype=jnp.int32) // (POOL * N_EXPERT)).astype(jnp.float32)
    fraction = data_pos / max(N_DP - 1, 1)
    noise = jax.random.normal(jax.random.fold_in(key, 34), (total_rows, D), jnp.float32)
    rising = jnp.exp(fraction * jnp.log(3.0))
    values = (0.5 * common[None, :] + noise) * scales[None, :] * rising[:, None]
    values = values / jnp.sqrt(ROWS * 1.0)
    return jnp.clip(values, -8.0, 8.0).astype(jnp.bfloat16)


def draw_route(key, part):
    blocks = N_DP * N_EXPERT * N_EXPERT
    block_keys = jax.random.split(jax.random.fold_in(key, 41), blocks)
    chosen = jax.vmap(lambda block_key: jax.random.permutation(block_key, POOL)[:CAP])(block_keys)
    return chosen.reshape(-1).astype(jnp.int32)


def draw_counts(key, part):
    sources = N_DP * N_EXPERT
    base = jax.random.randint(jax.random.fold_in(key, 51), (sources, N_EXPERT), CAP // 2, CAP + 1)
    full_group = jax.random.randint(jax.random.fold_in(key, 52), (), 0, N_DP)
    full_target = jax.random.randint(jax.random.fold_in(key, 53), (), 0, N_EXPERT)
    low_source = jax.random.randint(jax.random.fold_in(key, 54), (), 0, sources)
    source_ids = jnp.arange(sources, dtype=jnp.int32)[:, None]
    target_ids = jnp.arange(N_EXPERT, dtype=jnp.int32)[None, :]
    base = jnp.where((source_ids == low_source) & (target_ids == (full_target + 1) % N_EXPERT), CAP // 2, base)
    base = jnp.where((source_ids // N_EXPERT == full_group) & (target_ids == full_target), CAP, base)
    return base.astype(jnp.int32)


def block_levels(key, extent, shards, smallest, top_value):
    loudness = 1.0
    for dim, parts in shards:
        heights = jax.random.uniform(jax.random.fold_in(jax.random.fold_in(key, 6), dim), (parts,), jnp.float32, smallest / len(shards), top_value / len(shards))
        loudness = loudness * jnp.repeat(jnp.exp(heights), extent[dim] // parts).reshape((-1,) + (1,) * (len(extent) - 1 - dim))
    return loudness


def centred(key, dims, deviation, reach, shards=(), kind=jnp.bfloat16):
    drawn = jax.random.normal(key, dims, jnp.float32) * deviation
    if len(shards) > 0:
        drawn = block_levels(key, dims, shards, -0.22, 0.18) * drawn
    return jnp.clip(drawn, min=-reach, max=reach).astype(kind)


def setup_inputs(seed: int = 0) -> dict:
    splits = jax.random.split(jax.random.key(seed), 10)
    tokens = draw_tokens(jax.random.fold_in(splits[9], 71), 0)
    cotangent = draw_cotangent(jax.random.fold_in(splits[9], 71), 0)
    route = draw_route(jax.random.fold_in(splits[9], 71), 0)
    counts = draw_counts(jax.random.fold_in(splits[9], 71), 0)
    gate_master = centred(splits[4], (EXPERTS, D, FF), D ** -0.5, 0.125, ((0, 8), (1, 64)), jnp.float32)
    up_master = centred(splits[5], (EXPERTS, D, FF), D ** -0.5, 0.125, ((0, 8), (1, 64)), jnp.float32)
    down_master = centred(splits[6], (EXPERTS, D, FF), FF ** -0.5, 0.21875, ((0, 8), (1, 64)), jnp.float32)
    first_moment = centred(splits[7], (EXPERTS, 3, D, FF), 0.3, 2.0, ((0, 8), (2, 64)), jnp.float32)
    second_moment = jnp.clip(jnp.exp(math.log(1.0) - 4.6051702 * jax.random.uniform(splits[8], (EXPERTS, 3, D, FF), jnp.float32) ** block_levels(splits[8], (EXPERTS, 3, D, FF), ((0, 8), (2, 64)), -0.2, 0.2)), 0.01, 1.0)
    return {"tokens": tokens, "cotangent": cotangent, "route": route, "counts": counts, "gate_master": gate_master, "up_master": up_master, "down_master": down_master, "first_moment": first_moment, "second_moment": second_moment}


first_decay = 0.9
second_decay = 0.95
learn_rate = 0.01
adam_eps = 1e-08
weight_decay = 0.1
adam_count = 100.0
norm_eps = 1e-06

def rounded(values):
    return lax.optimization_barrier(values.astype(jnp.bfloat16)).astype(jnp.float32)

def adasum_tree(vectors):
    for level_index in range(LEVELS):
        paired = vectors.reshape((vectors.shape[0] // 2, 2) + vectors.shape[1:])
        lower = rounded(paired[:, 0])
        upper = rounded(paired[:, 1])
        cross = lax.optimization_barrier(jnp.sum(lower * upper, axis=(2, 3)))
        lower_square = lax.optimization_barrier(jnp.sum(lower * lower, axis=(2, 3)))
        upper_square = lax.optimization_barrier(jnp.sum(upper * upper, axis=(2, 3)))
        lower_coef = 1.0 - cross / (2.0 * (lower_square + norm_eps))
        upper_coef = 1.0 - cross / (2.0 * (upper_square + norm_eps))
        vectors = lower_coef[:, :, None, None] * lower + upper_coef[:, :, None, None] * upper
    return vectors[0]

def reference(tokens, cotangent, route, counts, gate_master, up_master, down_master, first_moment, second_moment):
    capacity = ROWS // N_EXPERT
    pooled = tokens.reshape(N_DP, N_EXPERT, POOL, D)
    pooled_grads = cotangent.reshape(N_DP, N_EXPERT, POOL, D)
    routes = route.reshape(N_DP, N_EXPERT, N_EXPERT, capacity)
    limits = counts.reshape(N_DP, N_EXPERT, N_EXPERT)
    live_slots = jnp.arange(capacity, dtype=jnp.int32)[None, None, None, :] < limits[..., None]
    data_ids = jnp.arange(N_DP, dtype=jnp.int32)[:, None, None]
    source_ids = jnp.arange(N_EXPERT, dtype=jnp.int32)[None, :, None]
    forward = jnp.zeros((N_DP, N_EXPERT, POOL, D), jnp.float32)
    combined_all = []
    weights_all = []
    first_all = []
    second_all = []
    for expert_index in range(N_EXPERT):
        slot_rows = routes[:, :, expert_index, :]
        slot_live = live_slots[:, :, expert_index, :]
        token_in = jnp.where(slot_live[..., None], pooled[data_ids, source_ids, slot_rows], 0).reshape(N_DP, ROWS, D)
        grad_in = jnp.where(slot_live[..., None], pooled_grads[data_ids, source_ids, slot_rows], 0).reshape(N_DP, ROWS, D)
        w_gate = gate_master[expert_index].astype(jnp.bfloat16)
        w_up = up_master[expert_index].astype(jnp.bfloat16)
        w_down = down_master[expert_index].astype(jnp.bfloat16)

        def local_pass(pair):
            token_rows, grad_rows = pair
            gate_pre = jnp.dot(token_rows, w_gate, preferred_element_type=jnp.float32)
            up_pre = jnp.dot(token_rows, w_up, preferred_element_type=jnp.float32)
            back_hidden = jnp.dot(grad_rows, w_down, preferred_element_type=jnp.float32)
            sigmoid_gate = jax.nn.sigmoid(gate_pre)
            active_gate = gate_pre * sigmoid_gate
            hidden_act = (active_gate * up_pre).astype(jnp.bfloat16)
            d_gate = (back_hidden * up_pre * sigmoid_gate * (1.0 + gate_pre * (1.0 - sigmoid_gate))).astype(jnp.bfloat16)
            d_up = (back_hidden * active_gate).astype(jnp.bfloat16)
            grads = jnp.stack([jnp.dot(token_rows.T, d_gate, preferred_element_type=jnp.float32), jnp.dot(token_rows.T, d_up, preferred_element_type=jnp.float32), jnp.dot(grad_rows.T, hidden_act, preferred_element_type=jnp.float32)])
            return (grads, hidden_act)
        grads_all, hidden_all = lax.map(local_pass, (token_in, grad_in))
        combined = adasum_tree(grads_all)
        masters = jnp.stack([gate_master[expert_index], up_master[expert_index], down_master[expert_index]])
        new_first = first_decay * first_moment[expert_index] + (1.0 - first_decay) * combined
        new_second = second_decay * second_moment[expert_index] + (1.0 - second_decay) * combined * combined
        first_hat = new_first / (1.0 - first_decay ** adam_count)
        second_hat = new_second / (1.0 - second_decay ** adam_count)
        new_masters = masters - learn_rate * (first_hat / (jnp.sqrt(second_hat) + adam_eps) + weight_decay * masters)
        new_down = new_masters[2].astype(jnp.bfloat16)

        def project(hidden_act):
            return jnp.dot(hidden_act, new_down.T, preferred_element_type=jnp.float32).astype(jnp.bfloat16)
        outputs = lax.map(project, hidden_all).reshape(N_DP, N_EXPERT, capacity, D)
        updates = jnp.where(slot_live[..., None], outputs.astype(jnp.float32), 0.0)
        forward = forward.at[data_ids, source_ids, slot_rows].add(updates)
        combined_all.append(combined)
        weights_all.append(new_masters)
        first_all.append(new_first)
        second_all.append(new_second)
    forward_out = forward.reshape(ALL_TOKENS, D).astype(jnp.bfloat16)
    return (jnp.stack(combined_all), jnp.stack(weights_all), jnp.stack(first_all), jnp.stack(second_all), forward_out)
```

```python
import functools

import jax
import jax.numpy as jnp
from jax import lax
from jax.experimental import pallas as pl
from jax.experimental.pallas import tpu as pltpu
from jax.sharding import Mesh
from jax.sharding import PartitionSpec as P

AXES = ("y", "t", "l", "x", "c")
DP = ("y", "t", "l")
EXPERT = ("x", "c")
MESH_ID = pl.DeviceIdType.MESH

first_decay = 0.9
second_decay = 0.95
learn_rate = 0.01
adam_eps = 1e-08
weight_decay = 0.1
adam_count = 100.0
norm_eps = 1e-06
ANY = pl.BlockSpec(memory_space=pl.ANY)
VMEM = pl.BlockSpec(memory_space=pltpu.VMEM)
DMA = pltpu.SemaphoreType.DMA


def place():
    return tuple(lax.axis_index(a) for a in AXES)


def remote(src, dst, send_sem, recv_sem, dev):
    return pltpu.make_async_remote_copy(
        src_ref=src,
        dst_ref=dst,
        send_sem=send_sem,
        recv_sem=recv_sem,
        device_id=dev,
        device_id_type=MESH_ID,
    )


def full(dev):
    return {a: dev[a] if a in dev else lax.axis_index(a) for a in AXES}


def is_self(dev):
    same = None
    for a in AXES:
        if a in dev:
            eq = lax.axis_index(a) == dev[a]
            same = eq if same is None else jnp.logical_and(same, eq)
    return same


def greet(others, maybe_self):
    barrier = pltpu.get_barrier_semaphore()
    for dev in others:
        pl.semaphore_signal(barrier, inc=1, device_id=dev, device_id_type=MESH_ID)
    for dev in maybe_self:
        pl.semaphore_signal(barrier, inc=1, device_id=dev, device_id_type=MESH_ID)
    pl.semaphore_wait(barrier, len(others) + len(maybe_self))


def send_or_copy(src, dst, send_sem, recv_sem, dev):
    mine = is_self(dev)

    @pl.when(mine)
    def _():
        pltpu.make_async_copy(src, dst, recv_sem).start()

    @pl.when(jnp.logical_not(mine))
    def _():
        remote(src, dst, send_sem, recv_sem, dev).start()


def wait_sent(src, dst, send_sem, recv_sem, dev):
    @pl.when(jnp.logical_not(is_self(dev)))
    def _():
        remote(src, dst, send_sem, recv_sem, dev).wait_send()


def landed(ref, recv_sem):
    pltpu.make_async_copy(ref, ref, recv_sem).wait()


def worker_of_rows(e):
    y, t, l, x, c = place()
    return {"t": e, "l": t % 2, "x": (t // 2 + e) % 4, "c": l}


def tree_place(x, t):
    return (x + 8 - t) % 4


def source_of_rows(s):
    y, t, l, x, c = place()
    return {"t": 2 * tree_place(x, t) + l, "l": c, "x": s // 2, "c": s % 2}


def row_x(x, t):
    return (x + 8 - t // 2 - 2 * (t % 2)) % 4


def relay_shift():
    t, c = lax.axis_index("t"), lax.axis_index("c")
    return (t + 2 * c) % 4


def relay_to():
    return {"x": (lax.axis_index("x") + relay_shift()) % 4}


def relay_from():
    return {"x": (lax.axis_index("x") + 4 - relay_shift()) % 4}


def block_expert():
    return 2 * relay_from()["x"] + lax.axis_index("c")


def worker_of_block(h):
    return {"t": block_expert(), "l": lax.axis_index("t") // 4, "c": h}


def sender_of_block(k):
    y, t, l, x, c = place()
    return {"t": 4 * l + row_x(x, t), "l": k, "c": t % 2}


def block_of_owner(h):
    y, t, l, x, c = place()
    return {"t": 2 * x + c, "l": t // 4, "x": relay_to()["x"], "c": h}


def owner_of_block(k):
    y, t, l, x, c = place()
    return {"t": 4 * l + row_x(x, t), "l": k, "x": t // 2, "c": t % 2}


def ring(axis, step):
    return {axis: (lax.axis_index(axis) + step) % 4}


def gather_peers():
    l = lax.axis_index("l")
    return [{"l": 1 - l}, ring("x", 1), ring("x", 3), ring("y", 1), ring("y", 3)]


def gather_swap(g, send, recv):
    y, t, l, x, c = place()
    mine = g.at[:, y, l, row_x(x, t)]
    swap = remote(mine, mine, send.at[0], recv.at[0], {"l": 1 - l})
    swap.start()
    return swap


def gather_block(g, swap, send, recv):
    y, t, l, x, c = place()
    rows = g.shape[4] // 2
    first, last = pl.ds(0, rows), pl.ds(rows, rows)
    swap.wait_send()
    landed(g.at[:, y, 1 - l, row_x(x, t)], recv.at[0])

    def start_ring(axis, parts, base):
        at = lax.axis_index(axis)
        for k, step in ((0, 1), (1, 3)):
            part = parts(at, 0, 2)
            remote(part, part, send.at[base + k], recv.at[base + k], ring(axis, step)).start()

    def relay_ring(axis, parts, base):
        at = lax.axis_index(axis)
        for k, step in ((0, 1), (1, 3)):
            came = (at + 4 - step) % 4
            landed(parts(came, 0, 2), recv.at[base + k])
            part = parts(came, k, 1)
            remote(part, part, send.at[base + 2 + k], recv.at[base + 2 + k], ring(axis, step)).start()

    def end_ring(axis, parts, base):
        at = lax.axis_index(axis)
        for k, step in ((0, 1), (1, 3)):
            part = parts(at, 0, 2)
            remote(part, part, send.at[base + k], recv.at[base + k], ring(axis, step)).wait_send()
            part = parts((at + 4 - step) % 4, k, 1)
            remote(part, part, send.at[base + 2 + k], recv.at[base + 2 + k], ring(axis, step)).wait_send()
            landed(parts((at + 2) % 4, k, 1), recv.at[base + 2 + k])

    def x_one(at, k, n):
        return g.at[:, y, pl.ds(k, n), row_x(at, t), first]

    def y_one(at, k, n):
        return g.at[:, at, pl.ds(k, n), row_x(x, t), last]

    def y_all(at, k, n):
        return g.at[:, at, pl.ds(k, n), :, first]

    def x_all(at, k, n):
        return g.at[:, :, pl.ds(k, n), row_x(at, t), last]

    for one, two, base in ((("x", x_one), ("y", y_one), 1), (("y", y_all), ("x", x_all), 9)):
        start_ring(*one, base)
        start_ring(*two, base + 4)
        relay_ring(*one, base)
        relay_ring(*two, base + 4)
        end_ring(*one, base)
        end_ring(*two, base + 4)


GATHER_SEMS = 17


def dispatch_kernel(tok, grd, wts, xt, xg, g, relay, s_row, r_row, s_fwd, r_fwd, s_rl, r_rl, s_wt, r_wt, s_g, r_g):
    y, t, l, x, c = place()
    other = {"c": 1 - c}
    greet(
        [other] + gather_peers(),
        [worker_of_rows(e) for e in range(8)]
        + [source_of_rows(s) for s in range(8)]
        + [worker_of_block(h) for h in range(2)]
        + [sender_of_block(k) for k in range(2)]
        + [relay_to(), relay_from()],
    )
    to_relay = (wts, relay, s_rl, r_rl, relay_to())
    send_or_copy(*to_relay)
    landed(relay, r_rl)
    chunk = g.at[:, y, t // 4, t % 4, pl.ds(pl.multiple_of(l * 32, 32), 32)]
    weight_sends = [(relay.at[h], chunk, s_wt.at[h], r_wt.at[l], worker_of_block(h)) for h in range(2)]
    for a in weight_sends:
        send_or_copy(*a)
    mine = g.at[:, y, l, row_x(x, t)]
    for k in range(2):
        landed(mine.at[:, pl.ds(32 * k, 32)], r_wt.at[k])
    swap = gather_swap(g, s_g, r_g)
    row_sends = []
    slot = 2 * x + c
    for src, dst, which in ((tok, xt, 0), (grd, xg, 1)):
        for e in range(8):
            row_sends.append(
                (src.at[e], dst.at[l, slot], s_row.at[which, e], r_row.at[which, slot], worker_of_rows(e))
            )
    for a in row_sends:
        send_or_copy(*a)
    gather_block(g, swap, s_g, r_g)
    forwards = []
    for dst, which in ((xt, 0), (xg, 1)):
        for s in range(8):
            landed(dst.at[c, s], r_row.at[which, s])
            f = remote(dst.at[c, s], dst.at[c, s], s_fwd.at[which, s], r_fwd.at[which, s], other)
            f.start()
            forwards.append(f)
    for a in [to_relay] + weight_sends + row_sends:
        wait_sent(*a)
    for f in forwards:
        f.wait_send()
    for dst, which in ((xt, 0), (xg, 1)):
        for s in range(8):
            landed(dst.at[1 - c, s], r_fwd.at[which, s])


PAIRS = [(i, k) for i in range(4) for k in range(i, 4)]
LAST = (((1,), (1,)), ((), ()))


def pair_kernel(xt, xg, hid, state, ft, fg, fh, relay, tile, lines, box, send, recv, own, sb, rb, s_rl, r_rl):
    y, t, l, x, c = place()
    across, other = {"l": 1 - l}, {"c": 1 - c}
    peers = small_peers(False)
    greet([across, other] + peers, [relay_to(), relay_from()])
    mine = 2 * l
    theirs = 2 * (1 - l)
    first, local, second = [], [], []
    for k, (src, dst) in enumerate(((xt, ft), (xg, fg))):
        for n in range(4):
            cols = pl.ds(256 * n, 256)
            theirs_half = pl.ds(pl.multiple_of(512 * n + (1 - l) * 256, 256), 256)
            my_half = pl.ds(pl.multiple_of(512 * n + l * 256, 256), 256)
            first.append(
                remote(src.at[c, :, theirs_half], dst.at[mine + c, :, cols], send.at[k, n], recv.at[k, n], across)
            )
            local.append(pltpu.make_async_copy(src.at[:, :, my_half], dst.at[pl.ds(mine, 2), :, cols], own.at[k, n]))
    first.append(remote(hid, fh.at[:, pl.ds(mine, 2)], send.at[2, 0], recv.at[2, 0], across))
    local.append(pltpu.make_async_copy(hid, fh.at[:, pl.ds(mine, 2)], own.at[2, 0]))
    for f in first:
        f.start()
    to_relay = (state, relay, s_rl, r_rl, relay_to())
    send_or_copy(*to_relay)
    for f in local:
        f.start()
    for k, dst in ((0, ft), (1, fg)):
        for n in range(4):
            piece = dst.at[theirs + c, :, pl.ds(256 * n, 256)]
            landed(piece, recv.at[k, n])
            f = remote(piece, piece, send.at[3 + k, n], recv.at[3 + k, n], other)
            f.start()
            second.append(f)
    for f in local:
        f.wait()
    landed(fh.at[:, pl.ds(theirs, 2)], recv.at[2, 0])
    for f in first:
        f.wait_send()
    wait_sent(*to_relay)
    landed(relay, r_rl)
    for f in second:
        f.wait_send()
    for k, dst in ((0, ft), (1, fg)):
        for n in range(4):
            landed(dst.at[theirs + 1 - c, :, pl.ds(256 * n, 256)], recv.at[3 + k, n])
    lines[...] = jnp.zeros_like(lines)
    for n, (i, k) in enumerate(PAIRS):
        both_t = lax.dot_general(ft[i], ft[k], LAST, preferred_element_type=jnp.float32)
        both_g = lax.dot_general(fg[i], fg[k], LAST, preferred_element_type=jnp.float32)
        for m, both in ((0, both_t), (1, both_t), (2, both_g)):
            inner = lax.dot_general(fh[m, i], fh[m, k], LAST, preferred_element_type=jnp.float32)
            lines[pl.ds(10 * m + n, 1), :] = jnp.sum(both * inner, axis=0, keepdims=True)
    total = jnp.broadcast_to(jnp.sum(lines[...], axis=1, keepdims=True), (32, 128))
    tile[...] = small_sum(total, box, peers, 2 * l + c, sb, rb)


def small_peers(with_x):
    y, t, l, x, c = place()
    out = []
    for dx in range(4 if with_x else 1):
        for dl in range(2):
            for dc in range(2):
                if dx + dl + dc > 0:
                    out.append({"x": (x + dx) % 4, "l": (l + dl) % 2, "c": (c + dc) % 2})
    return out


def small_sum(part, box, peers, at, send, recv):
    box[at] = part
    sends = []
    for k, dev in enumerate(peers):
        f = remote(box.at[at], box.at[at], send.at[k], recv.at[k], dev)
        f.start()
        sends.append(f)
    for k in range(len(peers)):
        landed(box.at[at], recv.at[k])
    for f in sends:
        f.wait_send()
    return jnp.sum(box[...], axis=0)


def gram_tile(r, lines):
    rows = r.shape[2]
    lines[...] = jnp.zeros_like(lines)
    for m in range(3):

        def step(i, accs, m=m):
            at = pl.ds(pl.multiple_of(i * 16, 16), 16)
            parts = [r[k, m, at, :].astype(jnp.float32) for k in range(4)]
            out = []
            for n, (i1, i2) in enumerate(PAIRS):
                prod = parts[i1] * parts[i2]
                out.append(accs[n] + (prod[:8] + prod[8:]))
            return tuple(out)

        zero = tuple(jnp.zeros((8, 384), jnp.float32) for _ in PAIRS)
        accs = lax.fori_loop(0, rows // 16, step, zero)
        for n, acc in enumerate(accs):
            line = jnp.sum(acc, axis=0, keepdims=True)
            lines[pl.ds(10 * m + n, 1), :] = line[:, :128] + line[:, 128:256] + line[:, 256:]
    return jnp.broadcast_to(jnp.sum(lines[...], axis=1, keepdims=True), (32, 128))


def ring_kernel(axis, *refs):
    if axis == "x":
        v, state, r, gram, got_state, relay, lines, box, sv, rv, own, sb, rb, ss, rs = refs
    else:
        v, r, gram, relay, lines, box, box2, sv, rv, own, sb, rb, sb2, rb2 = refs
    y, t, l, x, c = place()
    at = lax.axis_index(axis)
    rows = r.shape[2]
    peers = small_peers(True)
    up, down = ring(axis, 1), ring(axis, 3)
    others = [up, down] + peers
    maybe = []
    if axis == "x":
        maybe = [worker_of_block(h) for h in range(2)] + [sender_of_block(k) for k in range(2)]
    else:
        others = others + [ring("y", k) for k in range(1, 4)]
    greet(others, maybe)
    low, high = pl.ds(0, rows // 2), pl.ds(rows // 2, rows // 2)
    far, nxt, prv = (at + 2) % 4, (at + 1) % 4, (at + 3) % 4

    def part(p):
        return v.at[row_x(p, t) if axis == "x" else p]

    def slot(p):
        return r.at[tree_place(p, t) if axis == "x" else p]

    first = [
        remote(part(far).at[:, low], relay.at[0], sv.at[0], rv.at[0], up),
        remote(part(far).at[:, high], relay.at[1], sv.at[1], rv.at[1], down),
        remote(part(nxt), slot(at), sv.at[2], rv.at[2], up),
        remote(part(prv), slot(at), sv.at[3], rv.at[3], down),
    ]
    for f in first:
        f.start()
    keep = pltpu.make_async_copy(part(at), slot(at), own)
    keep.start()
    sends = []
    if axis == "x":
        piece = pl.ds(pl.multiple_of(l * 32, 32), 32)
        for h in range(2):
            sends.append((state.at[h], got_state.at[:, piece], ss.at[h], rs.at[l], worker_of_block(h)))
        for a in sends:
            send_or_copy(*a)
    landed(relay.at[0], rv.at[0])
    fwd_up = remote(relay.at[0], slot(prv).at[:, low], sv.at[4], rv.at[4], up)
    fwd_up.start()
    landed(relay.at[1], rv.at[1])
    fwd_down = remote(relay.at[1], slot(nxt).at[:, high], sv.at[5], rv.at[5], down)
    fwd_down.start()
    keep.wait()
    landed(slot(prv), rv.at[2])
    landed(slot(nxt), rv.at[3])
    landed(slot(far).at[:, low], rv.at[4])
    landed(slot(far).at[:, high], rv.at[5])
    for f in first + [fwd_up, fwd_down]:
        f.wait_send()
    total = small_sum(gram_tile(r, lines), box, peers, x * 4 + l * 2 + c, sb, rb)
    if axis == "y":
        total = small_sum(total, box2, [ring("y", k) for k in range(1, 4)], y, sb2, rb2)
    gram[...] = total
    if axis == "x":
        for a in sends:
            wait_sent(*a)
        for k in range(2):
            landed(got_state.at[:, pl.ds(32 * k, 32)], rs.at[k])


def final_kernel(mine, comb, hid, ret, got, g, part, came, rounded, own, s_g, r_g, s_c, r_c, s_p, r_p, s_y, r_y):
    y, t, l, x, c = place()
    other = {"c": 1 - c}
    greet(
        [other] + gather_peers(),
        [block_of_owner(h) for h in range(2)]
        + [owner_of_block(k) for k in range(2)]
        + [worker_of_rows(e) for e in range(8)]
        + [source_of_rows(s) for s in range(8)],
    )
    keep = pltpu.make_async_copy(mine, g.at[:, y, l, row_x(x, t)], own)
    keep.start()
    col = pl.ds(pl.multiple_of(c * 384, 384), 384)
    sends = []
    for k in range(2):
        sends.append(
            (
                comb.at[:, pl.ds(32 * k, 32)],
                got.at[:, :, col],
                s_c.at[k],
                r_c.at[c],
                owner_of_block(k),
            )
        )
    keep.wait()
    swap = gather_swap(g, s_g, r_g)
    for a in sends:
        send_or_copy(*a)
    gather_block(g, swap, s_g, r_g)
    for n in range(8):
        rows = g[0, n // 2, n % 2].reshape(256, 384)
        for k in range(2):
            block = lax.dot_general(hid[k], rows, LAST, preferred_element_type=jnp.float32)
            part[k, :, :, pl.ds(256 * n, 256)] = block.reshape(8, 16, 256)
    swaps = []
    for s in range(8):
        f = remote(part.at[1 - c, s], came.at[s], s_p.at[s], r_p.at[s], other)
        f.start()
        swaps.append(f)
    backs = []
    for s in range(8):
        landed(came.at[s], r_p.at[s])
        rounded[s] = (part[c, s] + came[s]).astype(jnp.bfloat16)
        a = (rounded.at[s], ret.at[t], s_y.at[s], r_y.at[t], source_of_rows(s))
        send_or_copy(*a)
        backs.append(a)
    for f in swaps:
        f.wait_send()
    for a in sends + backs:
        wait_sent(*a)
    for h in range(2):
        landed(got.at[:, :, pl.ds(384 * h, 384)], r_c.at[h])
    for e in range(8):
        landed(ret.at[e], r_y.at[e])


def call(kernel, outs, in_specs, out_specs, scratch, cid):
    return pl.pallas_call(
        kernel,
        out_shape=outs,
        in_specs=in_specs,
        out_specs=out_specs,
        scratch_shapes=scratch,
        compiler_params=pltpu.CompilerParams(
            collective_id=cid, has_side_effects=True, vmem_limit_bytes=48 * 1024 * 1024
        ),
    )


def shape(dims, kind=jnp.bfloat16):
    return jax.ShapeDtypeStruct(dims, kind)


def pair_coefs(cross, lower, upper):
    return (
        1.0 - cross / (2.0 * (lower + norm_eps)),
        1.0 - cross / (2.0 * (upper + norm_eps)),
    )


def quad_coefs(gram):
    a0, b0 = pair_coefs(gram[0][1], gram[0][0], gram[1][1])
    a1, b1 = pair_coefs(gram[2][3], gram[2][2], gram[3][3])
    lower = a0 * a0 * gram[0][0] + 2.0 * a0 * b0 * gram[0][1] + b0 * b0 * gram[1][1]
    upper = a1 * a1 * gram[2][2] + 2.0 * a1 * b1 * gram[2][3] + b1 * b1 * gram[3][3]
    cross = a0 * (a1 * gram[0][2] + b1 * gram[0][3]) + b0 * (a1 * gram[1][2] + b1 * gram[1][3])
    a2, b2 = pair_coefs(cross, lower, upper)
    return jnp.stack([a2 * a0, a2 * b0, b2 * a1, b2 * b1])


def tile_coefs(tile):
    sums = tile[:30, 0].reshape(3, 10)
    gram = [[None] * 4 for _ in range(4)]
    for n, (i, k) in enumerate(PAIRS):
        gram[i][k] = sums[:, n]
    return quad_coefs(gram)


def shards(
    tokens,
    cotangent,
    route,
    counts,
    gate_master,
    up_master,
    down_master,
    first_moment,
    second_moment,
):
    y, t, l, x, c = place()
    bf16, f32 = jnp.bfloat16, jnp.float32
    slot_ids = jnp.arange(128, dtype=jnp.int32)
    live_slots = slot_ids % 16 < jnp.repeat(counts[0], 16)
    sent_tokens = jnp.where(live_slots[:, None], jnp.take(tokens, route, axis=0), 0)
    sent_grads = jnp.where(live_slots[:, None], jnp.take(cotangent, route, axis=0), 0)
    masters = jnp.stack([gate_master[0], up_master[0], down_master[0]])
    halves = jnp.moveaxis(masters.astype(bf16).reshape(3, 32, 2, 384), 2, 0)
    xt, xg, weights, _ = call(
        dispatch_kernel,
        (
            shape((2, 8, 16, 2048)),
            shape((2, 8, 16, 2048)),
            shape((3, 4, 2, 4, 64, 384)),
            shape((2, 3, 32, 384)),
        ),
        [ANY] * 3,
        [ANY] * 4,
        [DMA((2, 8))] * 4 + [DMA(())] * 2 + [DMA((2,))] * 2 + [DMA((GATHER_SEMS,))] * 2,
        0,
    )(sent_tokens.reshape(8, 16, 2048), sent_grads.reshape(8, 16, 2048), halves)
    xt = xt.reshape(256, 2048)
    xg = xg.reshape(256, 2048)
    weights = weights.reshape(3, 2048, 384)
    gate_pre = jnp.dot(xt, weights[0], preferred_element_type=f32)
    up_pre = jnp.dot(xt, weights[1], preferred_element_type=f32)
    back_hidden = jnp.dot(xg, weights[2], preferred_element_type=f32)
    sigmoid_gate = jax.nn.sigmoid(gate_pre)
    active_gate = gate_pre * sigmoid_gate
    hidden = (active_gate * up_pre).astype(bf16)
    d_gate = (back_hidden * up_pre * sigmoid_gate * (1.0 + gate_pre * (1.0 - sigmoid_gate))).astype(bf16)
    d_up = (back_hidden * active_gate).astype(bf16)
    factors = jnp.stack([d_gate, d_up, hidden]).reshape(3, 2, 128, 384)
    state = jnp.stack([masters[2], first_moment[0, 2], second_moment[0, 2]])
    state = jnp.moveaxis(state.reshape(3, 32, 2, 384), 2, 0)
    four_t, four_g, four_h, state, tile = call(
        pair_kernel,
        (
            shape((4, 128, 1024)),
            shape((4, 128, 1024)),
            shape((3, 4, 128, 384)),
            shape((2, 3, 32, 384), f32),
            shape((32, 128), f32),
        ),
        [ANY] * 4,
        [VMEM] * 3 + [ANY, VMEM],
        [pltpu.VMEM((32, 128), f32), pltpu.VMEM((4, 32, 128), f32)]
        + [DMA((5, 4))] * 2
        + [DMA((3, 4))]
        + [DMA((3,))] * 2
        + [DMA(())] * 2,
        1,
    )(xt.reshape(2, 128, 2048), xg.reshape(2, 128, 2048), factors, state)
    coefs = tile_coefs(tile)
    four_t = four_t.reshape(512, 1024)
    four_g = four_g.reshape(512, 1024)
    scaled = four_h.astype(f32) * coefs.T[:, :, None, None]
    scaled = scaled.astype(bf16).reshape(3, 512, 384)
    rows_first = (((0,), (0,)), ((), ()))
    vec = jnp.stack(
        [
            lax.dot_general(src, scaled[m], rows_first, preferred_element_type=f32).astype(bf16)
            for m, src in ((0, four_t), (1, four_t), (2, four_g))
        ]
    )
    vec = jnp.moveaxis(vec.reshape(3, 4, 4, 64, 384), 2, 0).reshape(4, 3, 256, 384)
    got_x, tile, got_state = call(
        functools.partial(ring_kernel, "x"),
        (shape((4, 3, 256, 384)), shape((32, 128), f32), shape((3, 64, 384), f32)),
        [ANY, ANY],
        [VMEM, VMEM, ANY],
        [pltpu.VMEM((2, 3, 128, 384), bf16), pltpu.VMEM((32, 128), f32), pltpu.VMEM((16, 32, 128), f32)]
        + [DMA((6,)), DMA((6,)), DMA(())]
        + [DMA((15,))] * 2
        + [DMA((2,))] * 2,
        2,
    )(vec, state)
    coefs = tile_coefs(tile)
    vec = jnp.sum(got_x.astype(f32) * coefs[:, :, None, None], axis=0).astype(bf16)
    vec = jnp.moveaxis(vec.reshape(3, 4, 64, 384), 1, 0)
    got_y, tile = call(
        functools.partial(ring_kernel, "y"),
        (shape((4, 3, 64, 384)), shape((32, 128), f32)),
        [ANY],
        [VMEM, VMEM],
        [
            pltpu.VMEM((2, 3, 32, 384), bf16),
            pltpu.VMEM((32, 128), f32),
            pltpu.VMEM((16, 32, 128), f32),
            pltpu.VMEM((4, 32, 128), f32),
        ]
        + [DMA((6,)), DMA((6,)), DMA(())]
        + [DMA((15,))] * 2
        + [DMA((3,))] * 2,
        3,
    )(vec)
    coefs = tile_coefs(tile)
    part = jnp.sum(got_y.astype(f32) * coefs[:, :, None, None], axis=0)

    def adam(combined, weights, first, second):
        new_first = first_decay * first + (1.0 - first_decay) * combined
        new_second = second_decay * second + (1.0 - second_decay) * combined * combined
        first_hat = new_first / (1.0 - first_decay**adam_count)
        second_hat = new_second / (1.0 - second_decay**adam_count)
        new_weights = weights - learn_rate * (
            first_hat / (jnp.sqrt(second_hat) + adam_eps) + weight_decay * weights
        )
        return new_weights, new_first, new_second

    new_down = adam(part[2], got_state[0], got_state[1], got_state[2])[0].astype(bf16)
    returned, combined = call(
        final_kernel,
        (shape((8, 16, 2048)), shape((3, 32, 768), f32)),
        [ANY, ANY, VMEM],
        [ANY, ANY],
        [
            pltpu.VMEM((1, 4, 2, 4, 64, 384), bf16),
            pltpu.VMEM((2, 8, 16, 2048), f32),
            pltpu.VMEM((8, 16, 2048), f32),
            pltpu.VMEM((8, 16, 2048), bf16),
            DMA(()),
        ]
        + [DMA((GATHER_SEMS,))] * 2
        + [DMA((2,))] * 2
        + [DMA((8,))] * 4,
        4,
    )(new_down[None], part, hidden.reshape(2, 128, 384))
    pool_ids = jnp.arange(64, dtype=jnp.int32)
    selector = ((route[None, :] == pool_ids[:, None]) & live_slots[None, :]).astype(bf16)
    forward = jnp.dot(selector, returned.reshape(128, 2048), preferred_element_type=f32).astype(bf16)
    new_weights, new_first, new_second = adam(combined, masters, first_moment[0], second_moment[0])
    return (combined[None], new_weights[None], new_first[None], new_second[None], forward)


def solution(mesh):
    split = Mesh(mesh.devices.reshape(4, 8, 2, 4, 2), AXES)
    return jax.shard_map(
        shards,
        mesh=split,
        in_specs=(
            P(DP + EXPERT, None),
            P(DP + EXPERT, None),
            P(DP + EXPERT),
            P(DP + EXPERT, None),
            P(EXPERT, DP, None),
            P(EXPERT, DP, None),
            P(EXPERT, DP, None),
            P(EXPERT, None, DP, None),
            P(EXPERT, None, DP, None),
        ),
        out_specs=(
            P(EXPERT, None, DP, None),
            P(EXPERT, None, DP, None),
            P(EXPERT, None, DP, None),
            P(EXPERT, None, DP, None),
            P(DP + EXPERT, None),
        ),
        check_vma=False,
    )
```

```python
import jax
import jax.numpy as jnp
from jax import lax
from jax.experimental import pallas as pl
from jax.experimental.pallas import tpu as pltpu
from jax.sharding import Mesh
from jax.sharding import PartitionSpec as P

AXES = ("y", "t", "l", "x", "c")
DP = ("y", "t", "l")
EXPERT = ("x", "c")
MESH_ID = pl.DeviceIdType.MESH

first_decay = 0.9
second_decay = 0.95
learn_rate = 0.01
adam_eps = 1e-08
weight_decay = 0.1
adam_count = 100.0
norm_eps = 1e-06
ANY = pl.BlockSpec(memory_space=pl.ANY)
VMEM = pl.BlockSpec(memory_space=pltpu.VMEM)
DMA = pltpu.SemaphoreType.DMA


def place():
    return tuple(lax.axis_index(a) for a in AXES)


def remote(src, dst, send_sem, recv_sem, dev):
    return pltpu.make_async_remote_copy(
        src_ref=src,
        dst_ref=dst,
        send_sem=send_sem,
        recv_sem=recv_sem,
        device_id=dev,
        device_id_type=MESH_ID,
    )


def full(dev):
    return {a: dev[a] if a in dev else lax.axis_index(a) for a in AXES}


def is_self(dev):
    same = None
    for a in AXES:
        if a in dev:
            eq = lax.axis_index(a) == dev[a]
            same = eq if same is None else jnp.logical_and(same, eq)
    return same


def greet(others, maybe_self):
    barrier = pltpu.get_barrier_semaphore()
    for dev in others:
        pl.semaphore_signal(barrier, inc=1, device_id=dev, device_id_type=MESH_ID)
    for dev in maybe_self:
        pl.semaphore_signal(barrier, inc=1, device_id=dev, device_id_type=MESH_ID)
    pl.semaphore_wait(barrier, len(others) + len(maybe_self))


def send_or_copy(src, dst, send_sem, recv_sem, dev):
    mine = is_self(dev)

    @pl.when(mine)
    def _():
        pltpu.make_async_copy(src, dst, recv_sem).start()

    @pl.when(jnp.logical_not(mine))
    def _():
        remote(src, dst, send_sem, recv_sem, dev).start()


def wait_sent(src, dst, send_sem, recv_sem, dev):
    @pl.when(jnp.logical_not(is_self(dev)))
    def _():
        remote(src, dst, send_sem, recv_sem, dev).wait_send()


def landed(ref, recv_sem):
    pltpu.make_async_copy(ref, ref, recv_sem).wait()


def worker_of_rows(e):
    y, t, l, x, c = place()
    return {"t": e, "l": t % 2, "x": (t // 2 + e) % 4, "c": l}


def tree_place(x, t):
    return (x + 8 - t) % 4


def source_of_rows(s):
    y, t, l, x, c = place()
    return {"t": 2 * tree_place(x, t) + l, "l": c, "x": s // 2, "c": s % 2}


def row_x(x, t):
    return (x + 8 - t // 2 - 2 * (t % 2)) % 4


def relay_shift():
    t, c = lax.axis_index("t"), lax.axis_index("c")
    return (t + 2 * c) % 4


def relay_to():
    return {"x": (lax.axis_index("x") + relay_shift()) % 4}


def relay_from():
    return {"x": (lax.axis_index("x") + 4 - relay_shift()) % 4}


def block_expert():
    return 2 * relay_from()["x"] + lax.axis_index("c")


def worker_of_block(h):
    return {"t": block_expert(), "l": lax.axis_index("t") // 4, "c": h}


def sender_of_block(k):
    y, t, l, x, c = place()
    return {"t": 4 * l + row_x(x, t), "l": k, "c": t % 2}


def block_of_owner(h):
    y, t, l, x, c = place()
    return {"t": 2 * x + c, "l": t // 4, "x": relay_to()["x"], "c": h}


def owner_of_block(k):
    y, t, l, x, c = place()
    return {"t": 4 * l + row_x(x, t), "l": k, "x": t // 2, "c": t % 2}


def ring(axis, step):
    return {axis: (lax.axis_index(axis) + step) % 4}


def gather_peers():
    l = lax.axis_index("l")
    return [{"l": 1 - l}, ring("x", 1), ring("x", 3), ring("y", 1), ring("y", 3)]


def gather_swap(g, send, recv):
    y, t, l, x, c = place()
    mine = g.at[:, y, l, row_x(x, t)]
    swap = remote(mine, mine, send.at[0], recv.at[0], {"l": 1 - l})
    swap.start()
    return swap


def gather_steps(g, swap, send, recv):
    y, t, l, x, c = place()
    rows = g.shape[4] // 2
    first, last = pl.ds(0, rows), pl.ds(rows, rows)
    swap.wait_send()
    landed(g.at[:, y, 1 - l, row_x(x, t)], recv.at[0])

    def start_ring(axis, parts, base):
        at = lax.axis_index(axis)
        for k, step in ((0, 1), (1, 3)):
            part = parts(at, 0, 2)
            remote(part, part, send.at[base + k], recv.at[base + k], ring(axis, step)).start()

    def relay_ring(axis, parts, base):
        at = lax.axis_index(axis)
        for k, step in ((0, 1), (1, 3)):
            came = (at + 4 - step) % 4
            landed(parts(came, 0, 2), recv.at[base + k])
            part = parts(came, k, 1)
            remote(part, part, send.at[base + 2 + k], recv.at[base + 2 + k], ring(axis, step)).start()

    def end_ring(axis, parts, base):
        at = lax.axis_index(axis)
        for k, step in ((0, 1), (1, 3)):
            part = parts(at, 0, 2)
            remote(part, part, send.at[base + k], recv.at[base + k], ring(axis, step)).wait_send()
            part = parts((at + 4 - step) % 4, k, 1)
            remote(part, part, send.at[base + 2 + k], recv.at[base + 2 + k], ring(axis, step)).wait_send()
            landed(parts((at + 2) % 4, k, 1), recv.at[base + 2 + k])

    def x_one(at, k, n):
        return g.at[:, y, pl.ds(k, n), row_x(at, t), first]

    def y_one(at, k, n):
        return g.at[:, at, pl.ds(k, n), row_x(x, t), last]

    def y_all(at, k, n):
        return g.at[:, at, pl.ds(k, n), :, first]

    def x_all(at, k, n):
        return g.at[:, :, pl.ds(k, n), row_x(at, t), last]

    for one, two, base in ((("x", x_one), ("y", y_one), 1), (("y", y_all), ("x", x_all), 9)):
        start_ring(*one, base)
        start_ring(*two, base + 4)
        yield
        relay_ring(*one, base)
        relay_ring(*two, base + 4)
        yield
        end_ring(*one, base)
        end_ring(*two, base + 4)
        yield


def gather_block(g, swap, send, recv):
    for _ in gather_steps(g, swap, send, recv):
        pass


GATHER_SEMS = 17


EARLY = 4


def dispatch_kernel(
    tok, grd, wts, xt, xg, g, relay, xpt, xpg,
    s_row, r_row, s_fwd, r_fwd, s_rl, r_rl, s_wt, r_wt, s_g, r_g, s_x, r_x, s_xf, r_xf,
):
    y, t, l, x, c = place()
    other, across = {"c": 1 - c}, {"l": 1 - l}
    greet(
        [other] + gather_peers(),
        [worker_of_rows(e) for e in range(8)]
        + [source_of_rows(s) for s in range(8)]
        + [worker_of_block(h) for h in range(2)]
        + [sender_of_block(k) for k in range(2)]
        + [relay_to(), relay_from()],
    )
    to_relay = (wts, relay, s_rl, r_rl, relay_to())
    send_or_copy(*to_relay)
    row_sends = []
    slot = 2 * x + c
    for src, dst, which in ((tok, xt, 0), (grd, xg, 1)):
        for k, off in enumerate((4, 2, 6, 1, 7, 3, 5, 0)):
            e = (t + off) % 8
            row_sends.append(
                (src.at[e], dst.at[l, slot], s_row.at[which, k], r_row.at[which, slot], worker_of_rows(e))
            )
    for a in row_sends[:EARLY]:
        send_or_copy(*a)
    landed(relay, r_rl)
    chunk = g.at[:, y, t // 4, t % 4, pl.ds(pl.multiple_of(l * 32, 32), 32)]
    weight_sends = [(relay.at[h], chunk, s_wt.at[h], r_wt.at[l], worker_of_block(h)) for h in range(2)]
    for a in weight_sends:
        send_or_copy(*a)
    mine = g.at[:, y, l, row_x(x, t)]
    for k in range(2):
        landed(mine.at[:, pl.ds(32 * k, 32)], r_wt.at[k])
    swap = gather_swap(g, s_g, r_g)
    for a in row_sends[EARLY:8]:
        send_or_copy(*a)
    steps = gather_steps(g, swap, s_g, r_g)
    for _ in range(3):
        next(steps)
    for a in row_sends[8:]:
        send_or_copy(*a)
    next(steps)
    forwards, crossings = [], []

    def rows_in(dst, far, which):
        for s in range(8):
            part = dst.at[c, s]
            landed(part, r_row.at[which, s])
            f = remote(part, part, s_fwd.at[which, s], r_fwd.at[which, s], other)
            f.start()
            forwards.append(f)
        for n in range(4):
            cols = pl.ds(pl.multiple_of(512 * n + (1 - l) * 256, 256), 256)
            f = remote(
                dst.at[c, :, :, cols],
                far.at[c, :, :, pl.ds(256 * n, 256)],
                s_x.at[which, n],
                r_x.at[which, n],
                across,
            )
            f.start()
            crossings.append(f)

    def crossed(far, which):
        for n in range(4):
            piece = far.at[c, :, :, pl.ds(256 * n, 256)]
            landed(piece, r_x.at[which, n])
            f = remote(piece, piece, s_xf.at[which, n], r_xf.at[which, n], other)
            f.start()
            forwards.append(f)

    rows_in(xt, xpt, 0)
    next(steps)
    crossed(xpt, 0)
    rows_in(xg, xpg, 1)
    next(steps)
    for a in [to_relay] + weight_sends + row_sends:
        wait_sent(*a)
    crossed(xpg, 1)
    for f in forwards + crossings:
        f.wait_send()
    for dst, far, which in ((xt, xpt, 0), (xg, xpg, 1)):
        for s in range(8):
            landed(dst.at[1 - c, s], r_fwd.at[which, s])
        for n in range(4):
            landed(far.at[1 - c, :, :, pl.ds(256 * n, 256)], r_xf.at[which, n])


PAIRS = [(i, k) for i in range(4) for k in range(i, 4)]
LAST = (((1,), (1,)), ((), ()))


def small_peers(with_x):
    y, t, l, x, c = place()
    out = []
    for dx in range(4 if with_x else 1):
        for dl in range(2):
            for dc in range(2):
                if dx + dl + dc > 0:
                    out.append({"x": (x + dx) % 4, "l": (l + dl) % 2, "c": (c + dc) % 2})
    return out


def small_sum(part, box, peers, at, send, recv):
    box[at] = part
    sends = []
    for k, dev in enumerate(peers):
        f = remote(box.at[at], box.at[at], send.at[k], recv.at[k], dev)
        f.start()
        sends.append(f)
    for k in range(len(peers)):
        landed(box.at[at], recv.at[k])
    for f in sends:
        f.wait_send()
    return jnp.sum(box[...], axis=0)


def gram_tile(r, lines):
    rows = r.shape[2]
    lines[...] = jnp.zeros_like(lines)
    for m in range(3):

        def step(i, accs, m=m):
            at = pl.ds(pl.multiple_of(i * 16, 16), 16)
            parts = [r[k, m, at, :].astype(jnp.float32) for k in range(4)]
            out = []
            for n, (i1, i2) in enumerate(PAIRS):
                prod = parts[i1] * parts[i2]
                out.append(accs[n] + (prod[:8] + prod[8:]))
            return tuple(out)

        zero = tuple(jnp.zeros((8, 384), jnp.float32) for _ in PAIRS)
        accs = lax.fori_loop(0, rows // 16, step, zero)
        for n, acc in enumerate(accs):
            line = jnp.sum(acc, axis=0, keepdims=True)
            lines[pl.ds(10 * m + n, 1), :] = line[:, :128] + line[:, 128:256] + line[:, 256:]
    return jnp.broadcast_to(jnp.sum(lines[...], axis=1, keepdims=True), (32, 128))


def pair_coefs(cross, lower, upper):
    return (
        1.0 - cross / (2.0 * (lower + norm_eps)),
        1.0 - cross / (2.0 * (upper + norm_eps)),
    )


def quad_coefs(gram):
    a0, b0 = pair_coefs(gram[0][1], gram[0][0], gram[1][1])
    a1, b1 = pair_coefs(gram[2][3], gram[2][2], gram[3][3])
    lower = a0 * a0 * gram[0][0] + 2.0 * a0 * b0 * gram[0][1] + b0 * b0 * gram[1][1]
    upper = a1 * a1 * gram[2][2] + 2.0 * a1 * b1 * gram[2][3] + b1 * b1 * gram[3][3]
    cross = a0 * (a1 * gram[0][2] + b1 * gram[0][3]) + b0 * (a1 * gram[1][2] + b1 * gram[1][3])
    a2, b2 = pair_coefs(cross, lower, upper)
    return [a2 * a0, a2 * b0, b2 * a1, b2 * b1]


def tile_coefs(tile, m):
    gram = [[None] * 4 for _ in range(4)]
    for n, (i, k) in enumerate(PAIRS):
        gram[i][k] = tile[10 * m + n : 10 * m + n + 1, :]
    return [jnp.concatenate([w, w, w], axis=1) for w in quad_coefs(gram)]


def ring_exchange(axis, v, r, relay, part, slot, sv, rv, own):
    at = lax.axis_index(axis)
    rows = r.shape[2]
    up, down = ring(axis, 1), ring(axis, 3)
    low, high = pl.ds(0, rows // 2), pl.ds(rows // 2, rows // 2)
    far, nxt, prv = (at + 2) % 4, (at + 1) % 4, (at + 3) % 4
    first = [
        remote(v.at[part(far), :, low], relay.at[0], sv.at[0], rv.at[0], up),
        remote(v.at[part(far), :, high], relay.at[1], sv.at[1], rv.at[1], down),
        remote(v.at[part(nxt)], r.at[slot(at)], sv.at[2], rv.at[2], up),
        remote(v.at[part(prv)], r.at[slot(at)], sv.at[3], rv.at[3], down),
    ]
    for f in first:
        f.start()
    keep = pltpu.make_async_copy(v.at[part(at)], r.at[slot(at)], own)
    keep.start()
    landed(relay.at[0], rv.at[0])
    fwd_up = remote(relay.at[0], r.at[slot(prv), :, low], sv.at[4], rv.at[4], up)
    fwd_up.start()
    landed(relay.at[1], rv.at[1])
    fwd_down = remote(relay.at[1], r.at[slot(nxt), :, high], sv.at[5], rv.at[5], down)
    fwd_down.start()
    keep.wait()
    landed(r.at[slot(prv)], rv.at[2])
    landed(r.at[slot(nxt)], rv.at[3])
    landed(r.at[slot(far), :, low], rv.at[4])
    landed(r.at[slot(far), :, high], rv.at[5])
    for f in first + [fwd_up, fwd_down]:
        f.wait_send()


def adam(combined, weights, first, second):
    new_first = first_decay * first + (1.0 - first_decay) * combined
    new_second = second_decay * second + (1.0 - second_decay) * combined * combined
    first_hat = new_first / (1.0 - first_decay**adam_count)
    second_hat = new_second / (1.0 - second_decay**adam_count)
    new_weights = weights - learn_rate * (
        first_hat / (jnp.sqrt(second_hat) + adam_eps) + weight_decay * weights
    )
    return new_weights, new_first, new_second


def tree_kernel(
    xt, xg, xpt, xpg, hid, master, moment1, moment2,
    ret, got,
    ft, fg, fh, fs, gram, lines, relay, own_state, v, r, rel, vy, ry, rely, comb, g, part, came, rounded, via,
    box_a, box_b, box_c, box_d,
    own, s_h, r_h, s_rl, r_rl, s_st, r_st, sv, rv, sw, rw,
    s_a, r_a, s_b, r_b, s_c, r_c, s_d, r_d, s_g, r_g, s_o, r_o, s_p, r_p, s_y, r_y, s_z, r_z,
):
    y, t, l, x, c = place()
    across, other = {"l": 1 - l}, {"c": 1 - c}
    quad, wide = small_peers(False), small_peers(True)
    column = [ring("y", k) for k in range(1, 4)]
    row_home = [{"t": 2 * q + l, "l": k} for q in range(4) for k in range(2)]
    row_from = [{"t": e, "l": t % 2} for e in range(8)]
    row_via = [{"x": s // 2, "c": s % 2} for s in range(8)]
    mine = 2 * l
    theirs = 2 * (1 - l)
    local = [pltpu.make_async_copy(hid, fh.at[:, pl.ds(mine, 2)], own.at[8])]
    for k, (src, far, dst) in enumerate(((xt, xpt, ft), (xg, xpg, fg))):
        for n in range(4):
            cols = pl.ds(pl.multiple_of(512 * n + l * 256, 256), 256)
            local.append(
                pltpu.make_async_copy(
                    src.at[:, :, cols], dst.at[pl.ds(mine, 2), :, pl.ds(256 * n, 256)], own.at[4 * k + n]
                )
            )
        local.append(pltpu.make_async_copy(far, dst.at[pl.ds(theirs, 2)], own.at[9 + k]))
    for f in local:
        f.start()
    greet(
        quad + wide + column,
        [worker_of_block(h) for h in range(2)]
        + [sender_of_block(k) for k in range(2)]
        + [block_of_owner(h) for h in range(2)]
        + [owner_of_block(k) for k in range(2)]
        + [relay_to(), relay_from()]
        + row_home
        + row_from,
    )
    cross = remote(hid, fh.at[:, pl.ds(mine, 2)], s_h, r_h, across)
    cross.start()
    to_relay = [
        (src, relay.at[k], s_rl.at[k], r_rl.at[k], relay_to())
        for k, src in enumerate((master.at[0], moment1.at[0, 2], moment2.at[0, 2]))
    ]
    for a in to_relay:
        send_or_copy(*a)
    for f in local:
        f.wait()
    for k in range(3):
        landed(relay.at[k], r_rl.at[k])
    piece = pl.ds(pl.multiple_of(l * 32, 32), 32)
    state_sends = [
        (relay.at[:, :, pl.ds(384 * h, 384)], own_state.at[:, piece], s_st.at[h], r_st.at[l], worker_of_block(h)) for h in range(2)
    ]
    for a in state_sends:
        send_or_copy(*a)

    for n, (i, k) in enumerate(PAIRS):
        gram[0, n] = lax.dot_general(ft[i], ft[k], LAST, preferred_element_type=jnp.float32)
        gram[1, n] = lax.dot_general(fg[i], fg[k], LAST, preferred_element_type=jnp.float32)
    landed(fh.at[:, pl.ds(theirs, 2)], r_h)
    lines[...] = jnp.zeros_like(lines)
    for n, (i, k) in enumerate(PAIRS):
        for m in range(3):
            inner = lax.dot_general(fh[m, i], fh[m, k], LAST, preferred_element_type=jnp.float32)
            lines[pl.ds(10 * m + n, 1), :] = jnp.sum(gram[m // 2, n] * inner, axis=0, keepdims=True)
    total = jnp.broadcast_to(jnp.sum(lines[...], axis=1, keepdims=True), (32, 128))
    total = small_sum(total, box_a, quad, 2 * l + c, s_a, r_a)
    for m in range(3):
        for k, w in enumerate(tile_coefs(total, m)):
            fs[m, pl.ds(128 * k, 128), :] = (fh[m, k].astype(jnp.float32) * w).astype(jnp.bfloat16)
    for src, matrices in ((ft, (0, 1)), (fg, (2,))):
        for n in range(4):
            cols = src[:, :, pl.ds(256 * n, 256)].reshape(512, 256)
            for m in matrices:
                block = lax.dot_general(
                    cols, fs[m], (((0,), (0,)), ((), ())), preferred_element_type=jnp.float32
                ).astype(jnp.bfloat16)
                for q in range(4):
                    v[q, m, pl.ds(64 * n, 64), :] = block[64 * q : 64 * q + 64]

    ring_exchange("x", v, r, rel, lambda p: row_x(p, t), lambda p: tree_place(p, t), sv, rv, own.at[0])
    total = small_sum(gram_tile(r, lines), box_b, wide, x * 4 + l * 2 + c, s_b, r_b)
    for m in range(3):
        w = tile_coefs(total, m)
        for n in range(4):
            acc = r[0, m, pl.ds(64 * n, 64), :].astype(jnp.float32) * w[0]
            for k in range(1, 4):
                acc = acc + r[k, m, pl.ds(64 * n, 64), :].astype(jnp.float32) * w[k]
            vy[n, m] = acc.astype(jnp.bfloat16)

    ring_exchange("y", vy, ry, rely, lambda p: p, lambda p: p, sw, rw, own.at[1])
    total = small_sum(gram_tile(ry, lines), box_c, wide, x * 4 + l * 2 + c, s_c, r_c)
    total = small_sum(total, box_d, column, y, s_d, r_d)
    for k in range(2):
        landed(own_state.at[:, pl.ds(32 * k, 32)], r_st.at[k])
    for m in range(3):
        w = tile_coefs(total, m)
        acc = ry[0, m].astype(jnp.float32) * w[0]
        for k in range(1, 4):
            acc = acc + ry[k, m].astype(jnp.float32) * w[k]
        comb[m] = acc
    g[0, y, l, row_x(x, t)] = adam(comb[2], own_state[0], own_state[1], own_state[2])[0].astype(jnp.bfloat16)

    swap = gather_swap(g, s_g, r_g)
    half = pl.ds(pl.multiple_of(c * 384, 384), 384)
    owner_sends = [
        (comb.at[:, pl.ds(32 * k, 32)], got.at[:, :, half], s_o.at[k], r_o.at[c], owner_of_block(k)) for k in range(2)
    ]
    for a in owner_sends:
        send_or_copy(*a)
    gather_block(g, swap, s_g, r_g)
    for n in range(8):
        rows = g[0, n // 2, n % 2].reshape(256, 384)
        for k in range(2):
            block = lax.dot_general(fh[2, mine + k], rows, LAST, preferred_element_type=jnp.float32)
            part[k, :, :, pl.ds(256 * n, 256)] = block.reshape(8, 16, 256)
    swaps = []
    for s in range(8):
        f = remote(part.at[1 - c, s], came.at[s], s_p.at[s], r_p.at[s], other)
        f.start()
        swaps.append(f)
    backs = []
    slot = 2 * tree_place(x, t) + c
    for s in range(8):
        landed(came.at[s], r_p.at[s])
        rounded[s] = (part[c, s] + came[s]).astype(jnp.bfloat16)
        a = (rounded.at[s], via.at[slot], s_y.at[s], r_y.at[slot], row_via[s])
        send_or_copy(*a)
        backs.append(a)
    for q in range(8):
        landed(via.at[q], r_y.at[q])
        a = (via.at[q], ret.at[t], s_z.at[q], r_z.at[t], row_home[q])
        send_or_copy(*a)
        backs.append(a)
    cross.wait_send()
    for f in swaps:
        f.wait_send()
    for a in to_relay + state_sends + owner_sends + backs:
        wait_sent(*a)
    for h in range(2):
        landed(got.at[:, :, pl.ds(384 * h, 384)], r_o.at[h])
    for e in range(8):
        landed(ret.at[e], r_z.at[e])


def call(kernel, outs, in_specs, out_specs, scratch, cid):
    return pl.pallas_call(
        kernel,
        out_shape=outs,
        in_specs=in_specs,
        out_specs=out_specs,
        scratch_shapes=scratch,
        compiler_params=pltpu.CompilerParams(
            collective_id=cid, has_side_effects=True, vmem_limit_bytes=48 * 1024 * 1024
        ),
    )


def shape(dims, kind=jnp.bfloat16):
    return jax.ShapeDtypeStruct(dims, kind)


def shards(
    tokens,
    cotangent,
    route,
    counts,
    gate_master,
    up_master,
    down_master,
    first_moment,
    second_moment,
):
    y, t, l, x, c = place()
    bf16, f32 = jnp.bfloat16, jnp.float32
    slot_ids = jnp.arange(128, dtype=jnp.int32)
    live_slots = slot_ids % 16 < jnp.repeat(counts[0], 16)
    sent_tokens = jnp.where(live_slots[:, None], jnp.take(tokens, route, axis=0), 0)
    sent_grads = jnp.where(live_slots[:, None], jnp.take(cotangent, route, axis=0), 0)
    masters = jnp.stack([gate_master[0], up_master[0], down_master[0]])
    halves = jnp.moveaxis(masters.astype(bf16).reshape(3, 32, 2, 384), 2, 0)
    xt, xg, weights, _, xpt, xpg = call(
        dispatch_kernel,
        (
            shape((2, 8, 16, 2048)),
            shape((2, 8, 16, 2048)),
            shape((3, 4, 2, 4, 64, 384)),
            shape((2, 3, 32, 384)),
            shape((2, 8, 16, 1024)),
            shape((2, 8, 16, 1024)),
        ),
        [ANY] * 3,
        [ANY] * 6,
        [DMA((2, 8))] * 4 + [DMA(())] * 2 + [DMA((2,))] * 2 + [DMA((GATHER_SEMS,))] * 2 + [DMA((2, 4))] * 4,
        0,
    )(sent_tokens.reshape(8, 16, 2048), sent_grads.reshape(8, 16, 2048), halves)
    xt = xt.reshape(256, 2048)
    xg = xg.reshape(256, 2048)
    weights = weights.reshape(3, 2048, 384)
    gate_pre = jnp.dot(xt, weights[0], preferred_element_type=f32)
    up_pre = jnp.dot(xt, weights[1], preferred_element_type=f32)
    back_hidden = jnp.dot(xg, weights[2], preferred_element_type=f32)
    sigmoid_gate = jax.nn.sigmoid(gate_pre)
    active_gate = gate_pre * sigmoid_gate
    hidden = (active_gate * up_pre).astype(bf16)
    d_gate = (back_hidden * up_pre * sigmoid_gate * (1.0 + gate_pre * (1.0 - sigmoid_gate))).astype(bf16)
    d_up = (back_hidden * active_gate).astype(bf16)
    factors = jnp.stack([d_gate, d_up, hidden]).reshape(3, 2, 128, 384)
    box = pltpu.VMEM((16, 32, 128), f32)
    returned, combined = call(
        tree_kernel,
        (shape((8, 16, 2048)), shape((3, 32, 768), f32)),
        [ANY] * 8,
        [ANY] * 2,
        [
            pltpu.VMEM((4, 128, 1024), bf16),
            pltpu.VMEM((4, 128, 1024), bf16),
            pltpu.VMEM((3, 4, 128, 384), bf16),
            pltpu.VMEM((3, 512, 384), bf16),
            pltpu.VMEM((2, 10, 128, 128), f32),
            pltpu.VMEM((32, 128), f32),
            pltpu.VMEM((3, 32, 768), f32),
            pltpu.VMEM((3, 64, 384), f32),
            pltpu.VMEM((4, 3, 256, 384), bf16),
            pltpu.VMEM((4, 3, 256, 384), bf16),
            pltpu.VMEM((2, 3, 128, 384), bf16),
            pltpu.VMEM((4, 3, 64, 384), bf16),
            pltpu.VMEM((4, 3, 64, 384), bf16),
            pltpu.VMEM((2, 3, 32, 384), bf16),
            pltpu.VMEM((3, 64, 384), f32),
            pltpu.VMEM((1, 4, 2, 4, 64, 384), bf16),
            pltpu.VMEM((2, 8, 16, 2048), f32),
            pltpu.VMEM((8, 16, 2048), f32),
            pltpu.VMEM((8, 16, 2048), bf16),
            pltpu.VMEM((8, 16, 2048), bf16),
            pltpu.VMEM((4, 32, 128), f32),
            box,
            box,
            pltpu.VMEM((4, 32, 128), f32),
            DMA((11,)),
        ]
        + [DMA(())] * 2
        + [DMA((3,))] * 2
        + [DMA((2,))] * 2
        + [DMA((6,))] * 4
        + [DMA((3,))] * 2
        + [DMA((15,))] * 4
        + [DMA((3,))] * 2
        + [DMA((GATHER_SEMS,))] * 2
        + [DMA((2,))] * 2
        + [DMA((8,))] * 6,
        1,
    )(
        xt.reshape(2, 128, 2048),
        xg.reshape(2, 128, 2048),
        xpt.reshape(2, 128, 1024),
        xpg.reshape(2, 128, 1024),
        factors,
        down_master,
        first_moment,
        second_moment,
    )
    pool_ids = jnp.arange(64, dtype=jnp.int32)
    selector = ((route[None, :] == pool_ids[:, None]) & live_slots[None, :]).astype(bf16)
    forward = jnp.dot(selector, returned.reshape(128, 2048), preferred_element_type=f32).astype(bf16)
    new_weights, new_first, new_second = adam(combined, masters, first_moment[0], second_moment[0])
    return (combined[None], new_weights[None], new_first[None], new_second[None], forward)


def solution(mesh):
    split = Mesh(mesh.devices.reshape(4, 8, 2, 4, 2), AXES)
    return jax.shard_map(
        shards,
        mesh=split,
        in_specs=(
            P(DP + EXPERT, None),
            P(DP + EXPERT, None),
            P(DP + EXPERT),
            P(DP + EXPERT, None),
            P(EXPERT, DP, None),
            P(EXPERT, DP, None),
            P(EXPERT, DP, None),
            P(EXPERT, None, DP, None),
            P(EXPERT, None, DP, None),
        ),
        out_specs=(
            P(EXPERT, None, DP, None),
            P(EXPERT, None, DP, None),
            P(EXPERT, None, DP, None),
            P(EXPERT, None, DP, None),
            P(DP + EXPERT, None),
        ),
        check_vma=False,
    )
```

```python
import jax
import jax.numpy as jnp
from jax import lax
from jax.experimental import pallas as pl
from jax.experimental.pallas import tpu as pltpu
from jax.sharding import Mesh
from jax.sharding import PartitionSpec as P

AXES = ("y", "t", "l", "x", "c")
DP = ("y", "t", "l")
EXPERT = ("x", "c")
MESH_ID = pl.DeviceIdType.MESH

first_decay = 0.9
second_decay = 0.95
learn_rate = 0.01
adam_eps = 1e-08
weight_decay = 0.1
adam_count = 100.0
norm_eps = 1e-06
ANY = pl.BlockSpec(memory_space=pl.ANY)
VMEM = pl.BlockSpec(memory_space=pltpu.VMEM)
DMA = pltpu.SemaphoreType.DMA


def place():
    return tuple(lax.axis_index(a) for a in AXES)


def remote(src, dst, send_sem, recv_sem, dev):
    return pltpu.make_async_remote_copy(
        src_ref=src,
        dst_ref=dst,
        send_sem=send_sem,
        recv_sem=recv_sem,
        device_id=dev,
        device_id_type=MESH_ID,
    )


def full(dev):
    return {a: dev[a] if a in dev else lax.axis_index(a) for a in AXES}


def is_self(dev):
    same = None
    for a in AXES:
        if a in dev:
            eq = lax.axis_index(a) == dev[a]
            same = eq if same is None else jnp.logical_and(same, eq)
    return same


def greet(others, maybe_self):
    barrier = pltpu.get_barrier_semaphore()
    for dev in others:
        pl.semaphore_signal(barrier, inc=1, device_id=dev, device_id_type=MESH_ID)
    for dev in maybe_self:
        pl.semaphore_signal(barrier, inc=1, device_id=dev, device_id_type=MESH_ID)
    pl.semaphore_wait(barrier, len(others) + len(maybe_self))


def send_or_copy(src, dst, send_sem, recv_sem, dev):
    mine = is_self(dev)

    @pl.when(mine)
    def _():
        pltpu.make_async_copy(src, dst, recv_sem).start()

    @pl.when(jnp.logical_not(mine))
    def _():
        remote(src, dst, send_sem, recv_sem, dev).start()


def wait_sent(src, dst, send_sem, recv_sem, dev):
    @pl.when(jnp.logical_not(is_self(dev)))
    def _():
        remote(src, dst, send_sem, recv_sem, dev).wait_send()


def landed(ref, recv_sem):
    pltpu.make_async_copy(ref, ref, recv_sem).wait()


def worker_of_rows(e):
    y, t, l, x, c = place()
    return {"t": e, "l": t % 2, "x": (t // 2 + e) % 4, "c": l}


def tree_place(x, t):
    return (x + 8 - t) % 4


def source_of_rows(s):
    y, t, l, x, c = place()
    return {"t": 2 * tree_place(x, t) + l, "l": c, "x": s // 2, "c": s % 2}


def row_x(x, t):
    return (x + 8 - t // 2 - 2 * (t % 2)) % 4


def relay_shift():
    t, c = lax.axis_index("t"), lax.axis_index("c")
    return (t + 2 * c) % 4


def relay_to():
    return {"x": (lax.axis_index("x") + relay_shift()) % 4}


def relay_from():
    return {"x": (lax.axis_index("x") + 4 - relay_shift()) % 4}


def block_expert():
    return 2 * relay_from()["x"] + lax.axis_index("c")


def worker_of_block(h):
    return {"t": block_expert(), "l": lax.axis_index("t") // 4, "c": h}


def sender_of_block(k):
    y, t, l, x, c = place()
    return {"t": 4 * l + row_x(x, t), "l": k, "c": t % 2}


def block_of_owner(h):
    y, t, l, x, c = place()
    return {"t": 2 * x + c, "l": t // 4, "x": relay_to()["x"], "c": h}


def owner_of_block(k):
    y, t, l, x, c = place()
    return {"t": 4 * l + row_x(x, t), "l": k, "x": t // 2, "c": t % 2}


def ring(axis, step):
    return {axis: (lax.axis_index(axis) + step) % 4}


def gather_peers():
    l = lax.axis_index("l")
    return [{"l": 1 - l}, ring("x", 1), ring("x", 3), ring("y", 1), ring("y", 3)]


def gather_swap(g, send, recv):
    y, t, l, x, c = place()
    mine = g.at[:, y, l, row_x(x, t)]
    swap = remote(mine, mine, send.at[0], recv.at[0], {"l": 1 - l})
    swap.start()
    return swap


def gather_steps(g, swap, send, recv):
    y, t, l, x, c = place()
    rows = g.shape[4] // 2
    first, last = pl.ds(0, rows), pl.ds(rows, rows)
    swap.wait_send()
    landed(g.at[:, y, 1 - l, row_x(x, t)], recv.at[0])

    def start_ring(axis, parts, base):
        at = lax.axis_index(axis)
        for k, step in ((0, 1), (1, 3)):
            part = parts(at, 0, 2)
            remote(part, part, send.at[base + k], recv.at[base + k], ring(axis, step)).start()

    def relay_ring(axis, parts, base):
        at = lax.axis_index(axis)
        for k, step in ((0, 1), (1, 3)):
            came = (at + 4 - step) % 4
            landed(parts(came, 0, 2), recv.at[base + k])
            part = parts(came, k, 1)
            remote(part, part, send.at[base + 2 + k], recv.at[base + 2 + k], ring(axis, step)).start()

    def end_ring(axis, parts, base):
        at = lax.axis_index(axis)
        for k, step in ((0, 1), (1, 3)):
            part = parts(at, 0, 2)
            remote(part, part, send.at[base + k], recv.at[base + k], ring(axis, step)).wait_send()
            part = parts((at + 4 - step) % 4, k, 1)
            remote(part, part, send.at[base + 2 + k], recv.at[base + 2 + k], ring(axis, step)).wait_send()
            landed(parts((at + 2) % 4, k, 1), recv.at[base + 2 + k])

    def x_one(at, k, n):
        return g.at[:, y, pl.ds(k, n), row_x(at, t), first]

    def y_one(at, k, n):
        return g.at[:, at, pl.ds(k, n), row_x(x, t), last]

    def y_all(at, k, n):
        return g.at[:, at, pl.ds(k, n), :, first]

    def x_all(at, k, n):
        return g.at[:, :, pl.ds(k, n), row_x(at, t), last]

    for one, two, base in ((("x", x_one), ("y", y_one), 1), (("y", y_all), ("x", x_all), 9)):
        start_ring(*one, base)
        start_ring(*two, base + 4)
        yield
        relay_ring(*one, base)
        relay_ring(*two, base + 4)
        yield
        end_ring(*one, base)
        end_ring(*two, base + 4)
        yield


def gather_block(g, swap, send, recv):
    for _ in gather_steps(g, swap, send, recv):
        pass


GATHER_SEMS = 17


PAIRS = [(i, k) for i in range(4) for k in range(i, 4)]
LAST = (((1,), (1,)), ((), ()))


def small_peers(with_x):
    y, t, l, x, c = place()
    out = []
    for dx in range(4 if with_x else 1):
        for dl in range(2):
            for dc in range(2):
                if dx + dl + dc > 0:
                    out.append({"x": (x + dx) % 4, "l": (l + dl) % 2, "c": (c + dc) % 2})
    return out


def small_sum(part, box, peers, at, send, recv):
    box[at] = part
    sends = []
    for k, dev in enumerate(peers):
        f = remote(box.at[at], box.at[at], send.at[k], recv.at[k], dev)
        f.start()
        sends.append(f)
    for k in range(len(peers)):
        landed(box.at[at], recv.at[k])
    for f in sends:
        f.wait_send()
    return jnp.sum(box[...], axis=0)


def gram_tile(r, lines):
    rows = r.shape[2]
    lines[...] = jnp.zeros_like(lines)
    for m in range(3):

        def step(i, accs, m=m):
            at = pl.ds(pl.multiple_of(i * 16, 16), 16)
            parts = [r[k, m, at, :].astype(jnp.float32) for k in range(4)]
            out = []
            for n, (i1, i2) in enumerate(PAIRS):
                prod = parts[i1] * parts[i2]
                out.append(accs[n] + (prod[:8] + prod[8:]))
            return tuple(out)

        zero = tuple(jnp.zeros((8, 384), jnp.float32) for _ in PAIRS)
        accs = lax.fori_loop(0, rows // 16, step, zero)
        for n, acc in enumerate(accs):
            line = jnp.sum(acc, axis=0, keepdims=True)
            lines[pl.ds(10 * m + n, 1), :] = line[:, :128] + line[:, 128:256] + line[:, 256:]
    return jnp.broadcast_to(jnp.sum(lines[...], axis=1, keepdims=True), (32, 128))


def pair_coefs(cross, lower, upper):
    return (
        1.0 - cross / (2.0 * (lower + norm_eps)),
        1.0 - cross / (2.0 * (upper + norm_eps)),
    )


def quad_coefs(gram):
    a0, b0 = pair_coefs(gram[0][1], gram[0][0], gram[1][1])
    a1, b1 = pair_coefs(gram[2][3], gram[2][2], gram[3][3])
    lower = a0 * a0 * gram[0][0] + 2.0 * a0 * b0 * gram[0][1] + b0 * b0 * gram[1][1]
    upper = a1 * a1 * gram[2][2] + 2.0 * a1 * b1 * gram[2][3] + b1 * b1 * gram[3][3]
    cross = a0 * (a1 * gram[0][2] + b1 * gram[0][3]) + b0 * (a1 * gram[1][2] + b1 * gram[1][3])
    a2, b2 = pair_coefs(cross, lower, upper)
    return [a2 * a0, a2 * b0, b2 * a1, b2 * b1]


def tile_coefs(tile, m):
    gram = [[None] * 4 for _ in range(4)]
    for n, (i, k) in enumerate(PAIRS):
        gram[i][k] = tile[10 * m + n : 10 * m + n + 1, :]
    return [jnp.concatenate([w, w, w], axis=1) for w in quad_coefs(gram)]


def ring_exchange(axis, v, r, relay, part, slot, sv, rv, own):
    at = lax.axis_index(axis)
    rows = r.shape[2]
    up, down = ring(axis, 1), ring(axis, 3)
    low, high = pl.ds(0, rows // 2), pl.ds(rows // 2, rows // 2)
    far, nxt, prv = (at + 2) % 4, (at + 1) % 4, (at + 3) % 4
    first = [
        remote(v.at[part(far), :, low], relay.at[0], sv.at[0], rv.at[0], up),
        remote(v.at[part(far), :, high], relay.at[1], sv.at[1], rv.at[1], down),
        remote(v.at[part(nxt)], r.at[slot(at)], sv.at[2], rv.at[2], up),
        remote(v.at[part(prv)], r.at[slot(at)], sv.at[3], rv.at[3], down),
    ]
    for f in first:
        f.start()
    keep = pltpu.make_async_copy(v.at[part(at)], r.at[slot(at)], own)
    keep.start()
    landed(relay.at[0], rv.at[0])
    fwd_up = remote(relay.at[0], r.at[slot(prv), :, low], sv.at[4], rv.at[4], up)
    fwd_up.start()
    landed(relay.at[1], rv.at[1])
    fwd_down = remote(relay.at[1], r.at[slot(nxt), :, high], sv.at[5], rv.at[5], down)
    fwd_down.start()
    keep.wait()
    landed(r.at[slot(prv)], rv.at[2])
    landed(r.at[slot(nxt)], rv.at[3])
    landed(r.at[slot(far), :, low], rv.at[4])
    landed(r.at[slot(far), :, high], rv.at[5])
    for f in first + [fwd_up, fwd_down]:
        f.wait_send()


def adam(combined, weights, first, second):
    new_first = first_decay * first + (1.0 - first_decay) * combined
    new_second = second_decay * second + (1.0 - second_decay) * combined * combined
    first_hat = new_first / (1.0 - first_decay**adam_count)
    second_hat = new_second / (1.0 - second_decay**adam_count)
    new_weights = weights - learn_rate * (
        first_hat / (jnp.sqrt(second_hat) + adam_eps) + weight_decay * weights
    )
    return new_weights, new_first, new_second


def step_kernel(
    tok, grd, gate, up, down, moment1, moment2,
    ret, got,
    xt, xg, wts, relay_w, g3,
    ft, fg, fh, fs, gram, lines, relay, own_state, v, r, rel, vy, ry, rely, comb, g, part, came, rounded, via,
    box_a, box_b, box_c, box_d,
    s_row, r_row, s_fwd, r_fwd, s_rw, r_rw, s_wt, r_wt, s_g3, r_g3, s_x, r_x, s_xf, r_xf,
    own, s_h, r_h, s_rl, r_rl, s_st, r_st, sv, rv, sw, rw,
    s_a, r_a, s_b, r_b, s_c, r_c, s_d, r_d, s_g, r_g, s_o, r_o, s_p, r_p, s_y, r_y, s_z, r_z,
):
    y, t, l, x, c = place()
    across, other = {"l": 1 - l}, {"c": 1 - c}
    quad, wide = small_peers(False), small_peers(True)
    column = [ring("y", k) for k in range(1, 4)]
    row_home = [{"t": 2 * q + l, "l": k} for q in range(4) for k in range(2)]
    row_from = [{"t": e, "l": t % 2} for e in range(8)]
    mine = 2 * l
    theirs = 2 * (1 - l)
    for m, master in enumerate((gate, up, down)):
        wts[m] = master[0].astype(jnp.bfloat16)
    greet(
        wide + column,
        [worker_of_rows(e) for e in range(8)]
        + [source_of_rows(s) for s in range(8)]
        + [worker_of_block(h) for h in range(2)]
        + [sender_of_block(k) for k in range(2)]
        + [block_of_owner(h) for h in range(2)]
        + [owner_of_block(k) for k in range(2)]
        + [relay_to(), relay_from()]
        + row_home
        + row_from,
    )
    wts_relay = (wts, relay_w, s_rw, r_rw, relay_to())
    send_or_copy(*wts_relay)
    row_sends = []
    slot = 2 * x + c
    for src, dst, which in ((tok, xt, 0), (grd, xg, 1)):
        for k, off in enumerate((4, 2, 6, 1, 7, 3, 5, 0)):
            e = (t + off) % 8
            row_sends.append(
                (src.at[e], dst.at[l, slot], s_row.at[which, k], r_row.at[which, slot], worker_of_rows(e))
            )
    landed(relay_w, r_rw)
    chunk = g3.at[:, y, t // 4, t % 4, pl.ds(pl.multiple_of(l * 32, 32), 32)]
    weight_sends = [(relay_w.at[:, :, pl.ds(384 * h, 384)], chunk, s_wt.at[h], r_wt.at[l], worker_of_block(h)) for h in range(2)]
    for a in weight_sends:
        send_or_copy(*a)
    own_chunk = g3.at[:, y, l, row_x(x, t)]
    for k in range(2):
        landed(own_chunk.at[:, pl.ds(32 * k, 32)], r_wt.at[k])
    swap = gather_swap(g3, s_g3, r_g3)
    for a in row_sends[:8]:
        send_or_copy(*a)
    steps = gather_steps(g3, swap, s_g3, r_g3)
    for _ in range(3):
        next(steps)
    for a in row_sends[8:]:
        send_or_copy(*a)
    next(steps)
    forwards, crossings = [], []

    def rows_in(dst, far, which):
        for s in range(8):
            part = dst.at[c, s]
            landed(part, r_row.at[which, s])
            f = remote(part, part, s_fwd.at[which, s], r_fwd.at[which, s], other)
            f.start()
            forwards.append(f)
        for n in range(4):
            cols = pl.ds(pl.multiple_of(512 * n + (1 - l) * 256, 256), 256)
            f = remote(
                dst.at[c, :, :, cols],
                far.at[mine + c, :, :, pl.ds(256 * n, 256)],
                s_x.at[which, n],
                r_x.at[which, n],
                across,
            )
            f.start()
            crossings.append(f)

    def crossed(far, which):
        for n in range(4):
            piece = far.at[theirs + c, :, :, pl.ds(256 * n, 256)]
            landed(piece, r_x.at[which, n])
            f = remote(piece, piece, s_xf.at[which, n], r_xf.at[which, n], other)
            f.start()
            forwards.append(f)

    rows_in(xt, ft, 0)
    next(steps)
    crossed(ft, 0)
    rows_in(xg, fg, 1)
    next(steps)
    for a in [wts_relay] + weight_sends + row_sends:
        wait_sent(*a)
    crossed(fg, 1)
    for f in forwards + crossings:
        f.wait_send()
    for dst, far, which in ((xt, ft, 0), (xg, fg, 1)):
        for s in range(8):
            landed(dst.at[1 - c, s], r_fwd.at[which, s])
        for n in range(4):
            landed(far.at[theirs + 1 - c, :, :, pl.ds(256 * n, 256)], r_xf.at[which, n])

    local = []
    for k, (src, dst) in enumerate(((xt, ft), (xg, fg))):
        for n in range(4):
            cols = pl.ds(pl.multiple_of(512 * n + l * 256, 256), 256)
            local.append(
                pltpu.make_async_copy(
                    src.at[:, :, :, cols], dst.at[pl.ds(mine, 2), :, :, pl.ds(256 * n, 256)], own.at[4 * k + n]
                )
            )
    for f in local:
        f.start()
    to_relay = [
        (src, relay.at[k], s_rl.at[k], r_rl.at[k], relay_to())
        for k, src in enumerate((down.at[0], moment1.at[0, 2], moment2.at[0, 2]))
    ]
    for a in to_relay:
        send_or_copy(*a)
    rows_t, rows_g = xt[...].reshape(256, 2048), xg[...].reshape(256, 2048)
    gate_pre = jnp.dot(rows_t, g3[0].reshape(2048, 384), preferred_element_type=jnp.float32)
    up_pre = jnp.dot(rows_t, g3[1].reshape(2048, 384), preferred_element_type=jnp.float32)
    back_hidden = jnp.dot(rows_g, g3[2].reshape(2048, 384), preferred_element_type=jnp.float32)
    sigmoid_gate = jax.nn.sigmoid(gate_pre)
    active_gate = gate_pre * sigmoid_gate
    hidden = active_gate * up_pre
    d_gate = back_hidden * up_pre * sigmoid_gate * (1.0 + gate_pre * (1.0 - sigmoid_gate))
    d_up = back_hidden * active_gate
    for m, value in enumerate((d_gate, d_up, hidden)):
        fh[m, pl.ds(mine, 2)] = value.astype(jnp.bfloat16).reshape(2, 128, 384)
    factors = fh.at[:, pl.ds(mine, 2)]
    cross = remote(factors, factors, s_h, r_h, across)
    cross.start()
    for f in local:
        f.wait()
    for k in range(3):
        landed(relay.at[k], r_rl.at[k])
    piece = pl.ds(pl.multiple_of(l * 32, 32), 32)
    state_sends = [
        (relay.at[:, :, pl.ds(384 * h, 384)], own_state.at[:, piece], s_st.at[h], r_st.at[l], worker_of_block(h)) for h in range(2)
    ]
    for a in state_sends:
        send_or_copy(*a)

    for n, (i, k) in enumerate(PAIRS):
        gram[0, n] = lax.dot_general(ft[i].reshape(128, 1024), ft[k].reshape(128, 1024), LAST, preferred_element_type=jnp.float32)
        gram[1, n] = lax.dot_general(fg[i].reshape(128, 1024), fg[k].reshape(128, 1024), LAST, preferred_element_type=jnp.float32)
    landed(fh.at[:, pl.ds(theirs, 2)], r_h)
    lines[...] = jnp.zeros_like(lines)
    for n, (i, k) in enumerate(PAIRS):
        for m in range(3):
            inner = lax.dot_general(fh[m, i], fh[m, k], LAST, preferred_element_type=jnp.float32)
            lines[pl.ds(10 * m + n, 1), :] = jnp.sum(gram[m // 2, n] * inner, axis=0, keepdims=True)
    total = jnp.broadcast_to(jnp.sum(lines[...], axis=1, keepdims=True), (32, 128))
    total = small_sum(total, box_a, quad, 2 * l + c, s_a, r_a)
    for m in range(3):
        for k, w in enumerate(tile_coefs(total, m)):
            fs[m, pl.ds(128 * k, 128), :] = (fh[m, k].astype(jnp.float32) * w).astype(jnp.bfloat16)
    for src, matrices in ((ft, (0, 1)), (fg, (2,))):
        for n in range(4):
            cols = src[:, :, :, pl.ds(256 * n, 256)].reshape(512, 256)
            for m in matrices:
                block = lax.dot_general(
                    cols, fs[m], (((0,), (0,)), ((), ())), preferred_element_type=jnp.float32
                ).astype(jnp.bfloat16)
                for q in range(4):
                    v[q, m, pl.ds(64 * n, 64), :] = block[64 * q : 64 * q + 64]

    ring_exchange("x", v, r, rel, lambda p: row_x(p, t), lambda p: tree_place(p, t), sv, rv, own.at[0])
    total = small_sum(gram_tile(r, lines), box_b, wide, x * 4 + l * 2 + c, s_b, r_b)
    for m in range(3):
        w = tile_coefs(total, m)
        for n in range(4):
            acc = r[0, m, pl.ds(64 * n, 64), :].astype(jnp.float32) * w[0]
            for k in range(1, 4):
                acc = acc + r[k, m, pl.ds(64 * n, 64), :].astype(jnp.float32) * w[k]
            vy[n, m] = acc.astype(jnp.bfloat16)

    ring_exchange("y", vy, ry, rely, lambda p: p, lambda p: p, sw, rw, own.at[1])
    total = small_sum(gram_tile(ry, lines), box_c, wide, x * 4 + l * 2 + c, s_c, r_c)
    total = small_sum(total, box_d, column, y, s_d, r_d)
    for k in range(2):
        landed(own_state.at[:, pl.ds(32 * k, 32)], r_st.at[k])
    for m in range(3):
        w = tile_coefs(total, m)
        acc = ry[0, m].astype(jnp.float32) * w[0]
        for k in range(1, 4):
            acc = acc + ry[k, m].astype(jnp.float32) * w[k]
        comb[m] = acc
    g[0, y, l, row_x(x, t)] = adam(comb[2], own_state[0], own_state[1], own_state[2])[0].astype(jnp.bfloat16)

    swap = gather_swap(g, s_g, r_g)
    half = pl.ds(pl.multiple_of(c * 384, 384), 384)
    owner_sends = [
        (comb.at[:, pl.ds(32 * k, 32)], got.at[:, :, half], s_o.at[k], r_o.at[c], owner_of_block(k)) for k in range(2)
    ]
    for a in owner_sends:
        send_or_copy(*a)
    gather_block(g, swap, s_g, r_g)
    for n in range(8):
        rows = g[0, n // 2, n % 2].reshape(256, 384)
        for k in range(2):
            block = lax.dot_general(fh[2, mine + k], rows, LAST, preferred_element_type=jnp.float32)
            part[k, :, :, pl.ds(256 * n, 256)] = block.reshape(8, 16, 256)
    swaps, backs = [], []
    turn = 2 * tree_place(x, t)
    order = [(turn + k) % 8 for k in range(8)]
    for s in order:
        f = remote(part.at[1 - c, s], came.at[s], s_p.at[s], r_p.at[s], other)
        f.start()
        swaps.append(f)
    for s in order:
        landed(came.at[s], r_p.at[s])
        rounded[s] = (part[c, s] + came[s]).astype(jnp.bfloat16)
        a = (rounded.at[s], via.at[turn + c], s_y.at[s], r_y.at[turn + c], {"x": s // 2, "c": s % 2})
        send_or_copy(*a)
        backs.append(a)
    for k in range(4):
        q = (x + 4 - k) % 4
        for n in range(2):
            at = 2 * q + n
            landed(via.at[at], r_y.at[at])
            a = (via.at[at], ret.at[t], s_z.at[at], r_z.at[t], {"t": 2 * q + l, "l": n})
            send_or_copy(*a)
            backs.append(a)
    cross.wait_send()
    for f in swaps:
        f.wait_send()
    for a in to_relay + state_sends + owner_sends + backs:
        wait_sent(*a)
    for h in range(2):
        landed(got.at[:, :, pl.ds(384 * h, 384)], r_o.at[h])
    for e in range(8):
        landed(ret.at[e], r_z.at[e])


def call(kernel, outs, in_specs, out_specs, scratch, cid):
    return pl.pallas_call(
        kernel,
        out_shape=outs,
        in_specs=in_specs,
        out_specs=out_specs,
        scratch_shapes=scratch,
        compiler_params=pltpu.CompilerParams(
            collective_id=cid, has_side_effects=True, vmem_limit_bytes=48 * 1024 * 1024
        ),
    )


def shape(dims, kind=jnp.bfloat16):
    return jax.ShapeDtypeStruct(dims, kind)


def shards(
    tokens,
    cotangent,
    route,
    counts,
    gate_master,
    up_master,
    down_master,
    first_moment,
    second_moment,
):
    y, t, l, x, c = place()
    bf16, f32 = jnp.bfloat16, jnp.float32
    slot_ids = jnp.arange(128, dtype=jnp.int32)
    live_slots = slot_ids % 16 < jnp.repeat(counts[0], 16)
    sent_tokens = jnp.where(live_slots[:, None], jnp.take(tokens, route, axis=0), 0)
    sent_grads = jnp.where(live_slots[:, None], jnp.take(cotangent, route, axis=0), 0)
    masters = jnp.stack([gate_master[0], up_master[0], down_master[0]])
    box = pltpu.VMEM((16, 32, 128), f32)
    returned, combined = call(
        step_kernel,
        (shape((8, 16, 2048)), shape((3, 32, 768), f32)),
        [ANY] * 2 + [VMEM] * 3 + [ANY] * 2,
        [ANY] * 2,
        [
            pltpu.VMEM((2, 8, 16, 2048), bf16),
            pltpu.VMEM((2, 8, 16, 2048), bf16),
            pltpu.VMEM((3, 32, 768), bf16),
            pltpu.VMEM((3, 32, 768), bf16),
            pltpu.VMEM((3, 4, 2, 4, 64, 384), bf16),
            pltpu.VMEM((4, 8, 16, 1024), bf16),
            pltpu.VMEM((4, 8, 16, 1024), bf16),
            pltpu.VMEM((3, 4, 128, 384), bf16),
            pltpu.VMEM((3, 512, 384), bf16),
            pltpu.VMEM((2, 10, 128, 128), f32),
            pltpu.VMEM((32, 128), f32),
            pltpu.VMEM((3, 32, 768), f32),
            pltpu.VMEM((3, 64, 384), f32),
            pltpu.VMEM((4, 3, 256, 384), bf16),
            pltpu.VMEM((4, 3, 256, 384), bf16),
            pltpu.VMEM((2, 3, 128, 384), bf16),
            pltpu.VMEM((4, 3, 64, 384), bf16),
            pltpu.VMEM((4, 3, 64, 384), bf16),
            pltpu.VMEM((2, 3, 32, 384), bf16),
            pltpu.VMEM((3, 64, 384), f32),
            pltpu.VMEM((1, 4, 2, 4, 64, 384), bf16),
            pltpu.VMEM((2, 8, 16, 2048), f32),
            pltpu.VMEM((8, 16, 2048), f32),
            pltpu.VMEM((8, 16, 2048), bf16),
            pltpu.VMEM((8, 16, 2048), bf16),
            pltpu.VMEM((4, 32, 128), f32),
            box,
            box,
            pltpu.VMEM((4, 32, 128), f32),
        ]
        + [DMA((2, 8))] * 4
        + [DMA(())] * 2
        + [DMA((2,))] * 2
        + [DMA((GATHER_SEMS,))] * 2
        + [DMA((2, 4))] * 4
        + [DMA((8,))]
        + [DMA(())] * 2
        + [DMA((3,))] * 2
        + [DMA((2,))] * 2
        + [DMA((6,))] * 4
        + [DMA((3,))] * 2
        + [DMA((15,))] * 4
        + [DMA((3,))] * 2
        + [DMA((GATHER_SEMS,))] * 2
        + [DMA((2,))] * 2
        + [DMA((8,))] * 6,
        1,
    )(
        sent_tokens.reshape(8, 16, 2048),
        sent_grads.reshape(8, 16, 2048),
        gate_master,
        up_master,
        down_master,
        first_moment,
        second_moment,
    )
    pool_ids = jnp.arange(64, dtype=jnp.int32)
    selector = ((route[None, :] == pool_ids[:, None]) & live_slots[None, :]).astype(bf16)
    forward = jnp.dot(selector, returned.reshape(128, 2048), preferred_element_type=f32).astype(bf16)
    new_weights, new_first, new_second = adam(combined, masters, first_moment[0], second_moment[0])
    return (combined[None], new_weights[None], new_first[None], new_second[None], forward)


def solution(mesh):
    split = Mesh(mesh.devices.reshape(4, 8, 2, 4, 2), AXES)
    return jax.shard_map(
        shards,
        mesh=split,
        in_specs=(
            P(DP + EXPERT, None),
            P(DP + EXPERT, None),
            P(DP + EXPERT),
            P(DP + EXPERT, None),
            P(EXPERT, DP, None),
            P(EXPERT, DP, None),
            P(EXPERT, DP, None),
            P(EXPERT, None, DP, None),
            P(EXPERT, None, DP, None),
        ),
        out_specs=(
            P(EXPERT, None, DP, None),
            P(EXPERT, None, DP, None),
            P(EXPERT, None, DP, None),
            P(EXPERT, None, DP, None),
            P(DP + EXPERT, None),
        ),
        check_vma=False,
    )
```
